32 devices in a mesh: tm: 8 (over y, x, core), space: 4 (over z).
Axes of the slice: x: 2, y: 2, z: 4, core: 2. Of those that a mesh axis runs over, the one named last changes fastest.
Arguments:
- forcing: float32 [256, 32768], P('tm', 'space'), may hold values from -6 to 6
- op_main: bfloat16 [512, 64, 448], P('space'), may hold values from -0.1205 to 2.61
- op_mass: bfloat16 [512, 64, 448], P('space'), may hold values from -0.0401 to 1.045
- jacobi_inv: bfloat16 [512, 64, 64], P('space'), may hold values from -0.0301 to 0.635
Outputs:
- spec_real: float32 [256, 32768], P('tm', 'space')
- spec_imag: float32 [256, 32768], P('tm', 'space')
- time_field: float32 [256, 32768], P('tm', 'space')
The draws below stay inside these ranges and needn't reach their ends.
All inputs are finite; a program needn't handle non-finite values.
Results may differ from the reference program's by a relative error of at most 0.0058.
Values may be sent and summed in bfloat16 or wider, within the bound.
A program may use at most 128 MiB of HBM per device.

```python
import math
import jax
import jax.numpy as jnp
from jax import lax

L = 256
BS = 64
BX = 4
BY = 4
NZ = 32
NBLK = 512
NDOF = 32768


def block_draw(key, slot_count, diag_low, diag_high, near_bound, far_bound):
    key_diag, key_near, key_far = jax.random.split(key, 3)
    full_shape = (NBLK, BS, slot_count * BS)
    near_jitter = jax.random.uniform(key_near, full_shape, minval=-near_bound, maxval=near_bound)
    far_jitter = jax.random.uniform(key_far, full_shape, minval=-far_bound, maxval=far_bound)
    diag_values = jax.random.uniform(key_diag, (NBLK, BS), minval=diag_low, maxval=diag_high)
    column = lax.broadcasted_iota(jnp.int32, full_shape, 2)
    output_row = lax.broadcasted_iota(jnp.int32, full_shape, 1)
    jitter = jnp.where(column < BS, near_jitter, far_jitter)
    return jitter + jnp.where(column == output_row, diag_values[:, :, None], 0.0)


def draw_op_main(key, part):
    values = block_draw(jax.random.fold_in(key, 11), 7, 1.5, 2.5, 0.1, 0.12)
    return values.astype(jnp.bfloat16)


def draw_op_mass(key, part):
    values = block_draw(jax.random.fold_in(key, 12), 7, 0.5, 1.0, 0.04, 0.04)
    return values.astype(jnp.bfloat16)


def draw_jacobi_inv(key, part):
    values = block_draw(jax.random.fold_in(key, 13), 1, 0.3, 0.6, 0.03, 0.03)
    return values.astype(jnp.bfloat16)


def levels(stream_key, dims, pieces, smallest, largest):
    gain, own = 1.0, jax.random.fold_in(stream_key, 6)
    for axis_at, parts in pieces:
        heights = jnp.exp(jax.random.uniform(jax.random.fold_in(own, axis_at), (parts,), jnp.float32, smallest / len(pieces), largest / len(pieces)))
        gain = gain * jnp.repeat(heights, dims[axis_at] // parts).reshape([-1 if axis == axis_at else 1 for axis in range(len(dims))])
    return gain


def gaussian(rng, extent, spread, reach, cuts=(), kind=jnp.bfloat16):
    entries = jax.random.normal(rng, extent, jnp.float32) * spread
    if len(cuts) > 0:
        entries = levels(rng, extent, cuts, -0.22, 0.18) * entries
    return jnp.clip(entries, min=-reach, max=reach).astype(kind)


def setup_inputs(seed: int = 0) -> dict:
    key_list = jax.random.split(jax.random.key(seed), 5)
    return {
        "forcing": gaussian(key_list[0], (L, NDOF), 1.0, 6.0, ((0, 8), (1, 4)), jnp.float32),
        "op_main": draw_op_main(jax.random.fold_in(key_list[4], 71), 0),
        "op_mass": draw_op_mass(jax.random.fold_in(key_list[4], 71), 0),
        "jacobi_inv": draw_jacobi_inv(jax.random.fold_in(key_list[4], 71), 0),
    }


alpha_decay = 0.25
two_pi = 2.0 * math.pi


def neighbour_stack(field_low):
    row_count = field_low.shape[0]
    shaped = field_low.reshape(row_count, NZ, BY, BX, BS)
    padded = jnp.pad(shaped, ((0, 0), (1, 1), (1, 1), (1, 1), (0, 0)))
    neighbours = [
        padded[:, 1:-1, 1:-1, 1:-1],
        padded[:, 1:-1, 1:-1, :-2],
        padded[:, 1:-1, 1:-1, 2:],
        padded[:, 1:-1, :-2, 1:-1],
        padded[:, 1:-1, 2:, 1:-1],
        padded[:, :-2, 1:-1, 1:-1],
        padded[:, 2:, 1:-1, 1:-1],
    ]
    return jnp.stack(neighbours, axis=4).reshape(row_count, NBLK, 7 * BS)


def apply_block(matrix, field_low):
    row_count = field_low.shape[0]
    stacked = neighbour_stack(field_low)
    product = jnp.einsum("bok,rbk->rbo", matrix, stacked, precision=lax.Precision.HIGHEST)
    return product.reshape(row_count, NDOF)


def apply_inverse(matrix, field_low):
    row_count = field_low.shape[0]
    shaped = field_low.reshape(row_count, NBLK, BS)
    product = jnp.einsum("boi,rbi->rbo", matrix, shaped, precision=lax.Precision.HIGHEST)
    return product.reshape(row_count, NDOF)


def to_low(values):
    rounded = values.astype(jnp.bfloat16)
    rounded = lax.optimization_barrier(rounded)
    return rounded.astype(jnp.float32)


def reference(forcing, op_main, op_mass, jacobi_inv):
    step_ids = jnp.arange(L, dtype=jnp.int32)
    ratios = step_ids.astype(jnp.float32) / L
    scaled = forcing * jnp.power(jnp.float32(alpha_decay), ratios)[:, None]
    spectrum = jnp.fft.fft(scaled, axis=0, norm="ortho")
    rhs_parts = jnp.stack([jnp.real(spectrum), jnp.imag(spectrum)], axis=1).astype(jnp.float32)
    phases = step_ids.astype(jnp.float32) * (-two_pi / L)
    modulus = alpha_decay ** (1.0 / L)
    beta_re = (modulus * jnp.cos(phases)).reshape(L // 8, 8)
    beta_im = (modulus * jnp.sin(phases)).reshape(L // 8, 8)
    main_wide = op_main.astype(jnp.float32)
    mass_wide = op_mass.astype(jnp.float32)
    inv_wide = jacobi_inv.astype(jnp.float32)
    grouped = rhs_parts.reshape(L // 8, 8, 2, NDOF)

    def solve_group(packed):
        rhs_group, group_re, group_im = packed
        rhs_rows = rhs_group.reshape(16, NDOF)
        first_iter = apply_inverse(inv_wide, to_low(rhs_rows))
        first_low = to_low(first_iter)
        main_image = apply_block(main_wide, first_low).reshape(8, 2, NDOF)
        mass_image = apply_block(mass_wide, first_low).reshape(8, 2, NDOF)
        coef_re = group_re[:, None]
        coef_im = group_im[:, None]
        res_re = rhs_group[:, 0] - main_image[:, 0] + coef_re * mass_image[:, 0] - coef_im * mass_image[:, 1]
        res_im = rhs_group[:, 1] - main_image[:, 1] + coef_re * mass_image[:, 1] + coef_im * mass_image[:, 0]
        residue = jnp.stack([res_re, res_im], axis=1).reshape(16, NDOF)
        second_iter = first_iter + apply_inverse(inv_wide, to_low(residue))
        return second_iter.reshape(8, 2, NDOF)

    solution = lax.map(solve_group, (grouped, beta_re, beta_im)).reshape(L, 2, NDOF)
    combined = lax.complex(solution[:, 0], solution[:, 1])
    in_time = jnp.fft.ifft(combined, axis=0, norm="ortho")
    time_field = jnp.real(in_time).astype(jnp.float32) * jnp.power(jnp.float32(alpha_decay), -ratios)[:, None]
    return solution[:, 0], solution[:, 1], time_field
```

```python
import functools
import math

import jax
import jax.numpy as jnp
import numpy as np
from jax import lax
from jax.experimental import pallas as pl
from jax.experimental.pallas import tpu as pltpu
from jax.sharding import PartitionSpec as P

BS = 64
BX = 4
BY = 4
LINE = BX * BS

alpha_decay = 0.25
MESH = pl.DeviceIdType.MESH


def split_table(table):
    high = table.astype(jnp.bfloat16)
    low = (table - high.astype(np.float64)).astype(jnp.bfloat16)
    return np.stack([high, low])


def tables(length):
    half = length // 2
    ids = np.arange(length)
    freqs = np.arange(half)
    angles = 2.0 * math.pi * ((freqs[:, None] * ids[None, :]) % length) / length
    norm = 1.0 / math.sqrt(length)
    real_rows = np.cos(angles) * norm
    imag_rows = -np.sin(angles) * norm
    imag_rows[0] = np.where(ids % 2 == 0, norm, -norm)
    packed = np.concatenate([real_rows, imag_rows], axis=0)
    decay = alpha_decay ** (ids / length)
    forward = packed * decay[None, :]
    weight = np.full((length,), 2.0)
    weight[0] = 1.0
    weight[half] = 1.0
    inverse = (packed * weight[:, None]).T / decay[:, None]
    mirror = np.zeros((length, length))
    mirror[0, half] = 1.0
    for row in range(1, half):
        mirror[row, half - row] = 1.0
        mirror[half + row, length - row] = -1.0
    modulus = alpha_decay ** (1.0 / length)
    beta = modulus * np.exp(-2j * math.pi * freqs / length)
    beta_high = beta.real.copy()
    beta_high[0] = -modulus
    beta_cross = beta.imag.copy()
    beta_cross[0] = 0.0
    coefs = np.stack([beta.real, beta_high, beta_cross]).astype(np.float32)
    coefs = np.ascontiguousarray(np.broadcast_to(coefs[:, :, None], (3, half, 128)))
    return split_table(forward), split_table(inverse), mirror.astype(jnp.bfloat16), coefs


def place(rank, count):
    quarter = count // 4
    chip = rank // quarter
    return (chip ^ (chip >> 1)) * quarter + rank % quarter


def dot_nn(left, right):
    return jnp.dot(left, right, preferred_element_type=jnp.float32)


def dot_nt(left, right):
    return lax.dot_general(
        left, right, (((1,), (1,)), ((), ())), preferred_element_type=jnp.float32
    )


def kernel(
    tm, space, lines,
    forcing, op_main, op_mass, jacobi, fwd, inv, mir, coef,
    spec_out, time_out,
    wide, sends, cols, main_raw, mass_raw, jac_raw, pick, picked, picked_jac, fwd_v, inv_v, mir_v, weights, gains,
    field, rhs, first, acc, spec_v, time_v,
    load_sem, main_sem, mass_sem, jac_sem, chunk_sem, own_sem,
    send1, recv1, send2, recv2, send3, recv3, send4, recv4,
):
    bf16 = jnp.bfloat16
    me = lax.axis_index("tm")
    plane = lax.axis_index("space")
    steps = forcing.shape[0]
    length = steps * tm
    half = length // 2
    width = lines * LINE
    blocks = lines * BX
    reach = BY // lines
    total = tm * space
    spot = place(me, tm)
    order = plane * tm + spot
    hops = [d for m in range(1, reach + 1) for d in (m, -m)]

    def coords(position):
        return {"tm": place(lax.rem(position, tm), tm), "space": position // tm}

    chunks = []
    peers = list(range(tm - 1, -1, -1))
    for d in peers:
        begin = pl.multiple_of(place(me ^ d, tm) * width, width)
        copy = pltpu.make_async_copy(
            forcing.at[:, pl.ds(begin, width)], wide.at[d], chunk_sem.at[d]
        )
        copy.start()
        chunks.append(copy)
    groups = BS // 8

    def fetch(source, target, sem, g):
        span = pl.ds(pl.multiple_of(g * 8, 8), 8)
        return pltpu.make_async_copy(source.at[span], target.at[span], sem.at[g])

    loads = [
        pltpu.make_async_copy(fwd, fwd_v, load_sem.at[0]),
        pltpu.make_async_copy(inv, inv_v, load_sem.at[1]),
        pltpu.make_async_copy(mir, mir_v, load_sem.at[2]),
    ]
    for g in range(groups):
        fetch(jacobi, jac_raw, jac_sem, g).start()
    loads[0].start()
    for g in range(groups):
        fetch(op_main, main_raw, main_sem, g).start()
    for g in range(groups):
        fetch(op_mass, mass_raw, mass_sem, g).start()
    loads[1].start()
    loads[2].start()

    barrier = pltpu.get_barrier_semaphore()
    for d in range(1, tm):
        pl.semaphore_signal(barrier, 1, device_id={"tm": me ^ d, "space": plane}, device_id_type=MESH)
    for hop in hops:
        @pl.when(jnp.logical_and(order + hop >= 0, order + hop < total))
        def _():
            pl.semaphore_signal(barrier, 1, device_id=coords(order + hop), device_id_type=MESH)
    others = sum(
        jnp.where(jnp.logical_and(order + hop >= 0, order + hop < total), 1, 0) for hop in hops
    )
    pl.semaphore_wait(barrier, tm - 1 + others)

    row = pl.multiple_of(me * steps, steps)

    def exchange1(d):
        return pltpu.make_async_remote_copy(
            src_ref=sends.at[d], dst_ref=cols.at[pl.ds(row, steps), :],
            send_sem=send1.at[d], recv_sem=recv1.at[d],
            device_id={"tm": me ^ d, "space": plane}, device_id_type=MESH,
        )

    def arrival1(d):
        theirs = pl.multiple_of((me ^ d) * steps, steps)
        return pltpu.make_async_remote_copy(
            src_ref=sends.at[d], dst_ref=cols.at[pl.ds(theirs, steps), :],
            send_sem=send1.at[d], recv_sem=recv1.at[d],
            device_id={"tm": me ^ d, "space": plane}, device_id_type=MESH,
        )

    for d, copy in zip(peers, chunks):
        copy.wait()
        if d == 0:
            cols[pl.ds(row, steps), :] = wide[d].astype(bf16)
        else:
            sends[d] = wide[d].astype(bf16)
            exchange1(d).start()

    held = op_main.shape[2]
    pick_row = lax.broadcasted_iota(jnp.int32, (blocks * 8, 2 * held), 0)
    pick_col = lax.broadcasted_iota(jnp.int32, (blocks * 8, 2 * held), 1)
    late = jnp.where(pick_col >= held, 1, 0)
    same = pick_col - late * held == spot * blocks + pick_row // 8
    for p in range(4):
        hit = jnp.logical_and(same, pick_row % 8 == 2 * p + late)
        pick[p] = jnp.where(hit, 1.0, 0.0).astype(bf16)

    def gather(source, raw, sem, target):
        @pl.loop(0, groups)
        def _(g):
            fetch(source, raw, sem, g).wait()
            value = None
            for p in range(4):
                pair = jnp.concatenate([raw[g * 8 + 2 * p], raw[g * 8 + 2 * p + 1]], axis=1)
                term = dot_nt(pick[p], pair)
                value = term if value is None else value + term
            span = pl.ds(pl.multiple_of(g * 8, 8), 8)
            target[:, span, :] = value.reshape(blocks, 8, value.shape[1])

    zero = jnp.zeros((BS, BS), bf16)
    first_y = lax.rem(spot * lines, BY)

    def assemble(part):
        for i in range(lines):
            for x in range(BX):
                block = i * BX + x
                slot = [picked[block, :, s * BS:(s + 1) * BS].astype(bf16) for s in range(7)]
                span = pl.ds(part * LINE + x * BS, BS)
                along = {x: slot[0], x - 1: slot[1], x + 1: slot[2]}
                weights[i, 0, span, :] = jnp.concatenate(
                    [along.get(j, zero) for j in range(BX)], axis=1
                )
                below, above = slot[3], slot[4]
                if lines != BY:
                    y = first_y + i
                    below = jnp.where(y > 0, below, zero)
                    above = jnp.where(y < BY - 1, above, zero)
                for s, piece in ((1, below), (2, above), (3, slot[5]), (4, slot[6])):
                    weights[i, s, span, :] = jnp.concatenate(
                        [piece if j == x else zero for j in range(BX)], axis=1
                    )

    gather(jacobi, jac_raw, jac_sem, picked_jac)
    for i in range(lines):
        for x in range(BX):
            own = picked_jac[i * BX + x].astype(bf16)
            gains[i, pl.ds(x * BS, BS), :] = jnp.concatenate(
                [own if j == x else zero for j in range(BX)], axis=1
            )
    gather(op_main, main_raw, main_sem, picked)
    assemble(0)

    for hop in hops:
        @pl.when(jnp.logical_or(order - hop < 0, order - hop >= total))
        def _():
            field[pl.ds(BY - hop * lines, lines)] = jnp.zeros((lines, length, LINE), bf16)

    def halo(hop, i, target):
        index = hops.index(hop) * lines + i
        return pltpu.make_async_remote_copy(
            src_ref=field.at[BY + i], dst_ref=field.at[BY - hop * lines + i],
            send_sem=send2.at[index], recv_sem=recv2.at[index],
            device_id=coords(target), device_id_type=MESH,
        )

    loads[0].wait()
    for d in range(1, tm):
        arrival1(d).wait_recv()

    for i in range(lines):
        part = cols[:, i * LINE:(i + 1) * LINE]
        hat = dot_nn(fwd_v[0], part) + dot_nn(fwd_v[1], part)
        rhs[i] = hat
        image = dot_nt(hat.astype(bf16), gains[i])
        first[i] = image
        field[BY + i] = image.astype(bf16)
        for hop in hops:
            @pl.when(jnp.logical_and(order + hop >= 0, order + hop < total))
            def _():
                halo(hop, i, order + hop).start()

    gather(op_mass, mass_raw, mass_sem, picked)
    assemble(1)

    def outside(j):
        return j < 0 or j >= lines

    for i in range(lines):
        value = dot_nt(field[BY + i], weights[i, 0])
        for s, j in ((1, i - 1), (2, i + 1)):
            if not outside(j):
                value += dot_nt(field[BY + j], weights[i, s])
        acc[i] = value

    def arrive(hop, i):
        @pl.when(jnp.logical_and(order - hop >= 0, order - hop < total))
        def _():
            halo(hop, i, order - hop).wait_recv()

    if lines != BY:
        for hop in hops:
            for i in range(lines):
                arrive(hop, i)
    loads[1].wait()
    loads[2].wait()
    top = lax.broadcasted_iota(jnp.int32, (half, LINE), 0) == 0
    own_low = coef[0][:, :1]
    own_high = coef[1][:, :1]
    cross = coef[2][:, :1]
    seconds = []
    for i in range(lines):
        if lines == BY:
            arrive(1, i)
            arrive(-1, i)
        value = acc[i] + dot_nt(field[i], weights[i, 3])
        value += dot_nt(field[i + 2 * BY], weights[i, 4])
        if lines != BY:
            for s, j in ((1, i - 1), (2, i + 1)):
                if outside(j):
                    value += dot_nt(field[BY + j], weights[i, s])
        mass_re = value[:half, LINE:]
        mass_im = value[half:, LINE:]
        res_re = rhs[i, :half] - value[:half, :LINE] + own_low * mass_re - cross * mass_im
        res_im = rhs[i, half:] - value[half:, :LINE] + own_high * mass_im + cross * mass_re
        residue = jnp.concatenate([res_re.astype(bf16), res_im.astype(bf16)], axis=0)
        second = first[i] + dot_nt(residue, gains[i])
        first[i] = second
        high = second.astype(bf16)
        mirrored = dot_nn(mir_v[...], high).astype(bf16)
        span = slice(i * LINE, (i + 1) * LINE)
        spec_v[0, :half, span] = high[:half]
        spec_v[0, half:, span] = mirrored[:half]
        spec_v[1, :half, span] = jnp.where(top, 0.0, second[half:]).astype(bf16)
        spec_v[1, half:, span] = mirrored[half:]

    mine = pl.multiple_of(spot * width, width)

    def exchange3(d, begin):
        theirs = pl.multiple_of((me ^ d) * steps, steps)
        return pltpu.make_async_remote_copy(
            src_ref=spec_v.at[:, pl.ds(theirs, steps), :],
            dst_ref=spec_out.at[:, :, pl.ds(begin, width)],
            send_sem=send3.at[d], recv_sem=recv3.at[d],
            device_id={"tm": me ^ d, "space": plane}, device_id_type=MESH,
        )

    def exchange4(d, begin):
        theirs = pl.multiple_of((me ^ d) * steps, steps)
        return pltpu.make_async_remote_copy(
            src_ref=time_v.at[pl.ds(theirs, steps), :],
            dst_ref=time_out.at[:, pl.ds(begin, width)],
            send_sem=send4.at[d], recv_sem=recv4.at[d],
            device_id={"tm": me ^ d, "space": plane}, device_id_type=MESH,
        )

    for d in range(tm - 1, 0, -1):
        exchange3(d, mine).start()
    own_spec = pltpu.make_async_copy(
        spec_v.at[:, pl.ds(row, steps), :], spec_out.at[:, :, pl.ds(mine, width)], own_sem.at[0]
    )
    own_spec.start()
    for i in range(lines):
        second = first[i]
        high = second.astype(bf16)
        low = (second - high.astype(jnp.float32)).astype(bf16)
        value = dot_nn(inv_v[0], high) + dot_nn(inv_v[1], high) + dot_nn(inv_v[0], low)
        time_v[:, i * LINE:(i + 1) * LINE] = value.astype(bf16)
    for d in range(tm - 1, 0, -1):
        exchange4(d, mine).start()
    own_time = pltpu.make_async_copy(
        time_v.at[pl.ds(row, steps), :], time_out.at[:, pl.ds(mine, width)], own_sem.at[1]
    )
    own_time.start()

    for d in range(1, tm):
        exchange1(d).wait_send()
    for hop in hops:
        @pl.when(jnp.logical_and(order + hop >= 0, order + hop < total))
        def _():
            for i in range(lines):
                halo(hop, i, order + hop).wait_send()
    own_spec.wait()
    own_time.wait()
    for d in range(1, tm):
        theirs = pl.multiple_of(place(me ^ d, tm) * width, width)
        exchange3(d, theirs).wait_recv()
        exchange4(d, theirs).wait_recv()
        exchange3(d, mine).wait_send()
        exchange4(d, mine).wait_send()


def per_device(tm, space, forcing, op_main, op_mass, jacobi_inv):
    steps, dofs = forcing.shape
    length = steps * tm
    half = length // 2
    lines = dofs // tm // LINE
    width = lines * LINE
    blocks = lines * BX
    held = op_main.shape[0]
    halos = 2 * (BY // lines) * lines
    bf16, f32 = jnp.bfloat16, jnp.float32
    forward, inverse, mirror, coefs = tables(length)
    any_space = pl.BlockSpec(memory_space=pl.ANY)
    vmem = pl.BlockSpec(memory_space=pltpu.VMEM)
    dma = pltpu.SemaphoreType.DMA
    spec, field = pl.pallas_call(
        functools.partial(kernel, tm, space, lines),
        out_shape=(
            jax.ShapeDtypeStruct((2, steps, dofs), bf16),
            jax.ShapeDtypeStruct((steps, dofs), bf16),
        ),
        in_specs=[any_space] * 7 + [vmem],
        out_specs=(any_space, any_space),
        scratch_shapes=[
            pltpu.VMEM((tm, steps, width), f32),
            pltpu.VMEM((tm, steps, width), bf16),
            pltpu.VMEM((length, width), bf16),
            pltpu.VMEM((BS, 7 * BS, held), bf16),
            pltpu.VMEM((BS, 7 * BS, held), bf16),
            pltpu.VMEM((BS, BS, held), bf16),
            pltpu.VMEM((4, blocks * 8, 2 * held), bf16),
            pltpu.VMEM((blocks, BS, 7 * BS), f32),
            pltpu.VMEM((blocks, BS, BS), f32),
            pltpu.VMEM((2, length, length), bf16),
            pltpu.VMEM((2, length, length), bf16),
            pltpu.VMEM((length, length), bf16),
            pltpu.VMEM((lines, 5, 2 * LINE, LINE), bf16),
            pltpu.VMEM((lines, LINE, LINE), bf16),
            pltpu.VMEM((lines + 2 * BY, length, LINE), bf16),
            pltpu.VMEM((lines, length, LINE), f32),
            pltpu.VMEM((lines, length, LINE), f32),
            pltpu.VMEM((lines, length, 2 * LINE), f32),
            pltpu.VMEM((2, length, width), bf16),
            pltpu.VMEM((length, width), bf16),
            dma((3,)), dma((BS // 8,)), dma((BS // 8,)), dma((BS // 8,)), dma((tm,)), dma((2,)),
            dma((tm,)), dma((tm,)),
            dma((halos,)), dma((halos,)),
            dma((tm,)), dma((tm,)),
            dma((tm,)), dma((tm,)),
        ],
        compiler_params=pltpu.CompilerParams(
            collective_id=0, has_side_effects=True, vmem_limit_bytes=56 * 1024 * 1024
        ),
    )(
        forcing, *(jnp.transpose(op, (1, 2, 0)) for op in (op_main, op_mass, jacobi_inv)),
        jnp.asarray(forward), jnp.asarray(inverse), jnp.asarray(mirror), jnp.asarray(coefs),
    )
    return spec[0].astype(f32), spec[1].astype(f32), field.astype(f32)


def solution(mesh):
    in_specs = (
        P("tm", "space"),
        P("space", None, None),
        P("space", None, None),
        P("space", None, None),
    )
    out_specs = (P("tm", "space"), P("tm", "space"), P("tm", "space"))
    body = functools.partial(per_device, mesh.shape["tm"], mesh.shape["space"])
    return jax.shard_map(
        body, mesh=mesh, in_specs=in_specs, out_specs=out_specs, check_vma=False
    )
```

```python
import functools
import math

import jax
import jax.numpy as jnp
import numpy as np
from jax import lax
from jax.experimental import pallas as pl
from jax.experimental.pallas import tpu as pltpu
from jax.sharding import PartitionSpec as P

BS = 64
BX = 4
BY = 4
LINE = BX * BS

alpha_decay = 0.25
MESH = pl.DeviceIdType.MESH


def split_table(table):
    high = table.astype(jnp.bfloat16)
    low = (table - high.astype(np.float64)).astype(jnp.bfloat16)
    return np.stack([high, low])


def tables(length):
    half = length // 2
    ids = np.arange(length)
    freqs = np.arange(half)
    angles = 2.0 * math.pi * ((freqs[:, None] * ids[None, :]) % length) / length
    norm = 1.0 / math.sqrt(length)
    real_rows = np.cos(angles) * norm
    imag_rows = -np.sin(angles) * norm
    imag_rows[0] = np.where(ids % 2 == 0, norm, -norm)
    packed = np.concatenate([real_rows, imag_rows], axis=0)
    decay = alpha_decay ** (ids / length)
    forward = packed * decay[None, :]
    weight = np.full((length,), 2.0)
    weight[0] = 1.0
    weight[half] = 1.0
    inverse = (packed * weight[:, None]).T / decay[:, None]
    mirror = np.zeros((length, length))
    mirror[0, half] = 1.0
    for row in range(1, half):
        mirror[row, half - row] = 1.0
        mirror[half + row, length - row] = -1.0
    modulus = alpha_decay ** (1.0 / length)
    beta = modulus * np.exp(-2j * math.pi * freqs / length)
    beta_high = beta.real.copy()
    beta_high[0] = -modulus
    beta_cross = beta.imag.copy()
    beta_cross[0] = 0.0
    coefs = np.stack([beta.real, beta_high, beta_cross]).astype(np.float32)
    coefs = np.ascontiguousarray(np.broadcast_to(coefs[:, :, None], (3, half, 128)))
    return split_table(forward), split_table(inverse), mirror.astype(jnp.bfloat16), coefs


def place(rank, count):
    quarter = count // 4
    chip = rank // quarter
    return (chip ^ (chip >> 1)) * quarter + rank % quarter


def dot_nn(left, right):
    return jnp.dot(left, right, preferred_element_type=jnp.float32)


def dot_nt(left, right):
    return lax.dot_general(
        left, right, (((1,), (1,)), ((), ())), preferred_element_type=jnp.float32
    )


def kernel(
    tm, space, lines,
    forcing, op_main, op_mass, jacobi, fwd, inv, mir, coef,
    out,
    wide, sends, cols, main_raw, mass_raw, jac_raw, pick, picked, picked_jac, fwd_v, inv_v, mir_v, weights, gains,
    field, rhs, first, acc, out_v,
    load_sem, main_sem, mass_sem, jac_sem, chunk_sem, own_sem,
    send1, recv1, send2, recv2, send3, recv3,
):
    bf16 = jnp.bfloat16
    me = lax.axis_index("tm")
    plane = lax.axis_index("space")
    steps = forcing.shape[0]
    length = steps * tm
    half = length // 2
    width = lines * LINE
    blocks = lines * BX
    reach = BY // lines
    total = tm * space
    spot = place(me, tm)
    order = plane * tm + spot
    hops = [d for m in range(1, reach + 1) for d in (m, -m)]

    def coords(position):
        return {"tm": place(lax.rem(position, tm), tm), "space": position // tm}

    chunks = []
    peers = list(range(tm - 1, -1, -1))
    for d in peers:
        begin = pl.multiple_of(place(me ^ d, tm) * width, width)
        copy = pltpu.make_async_copy(
            forcing.at[:, pl.ds(begin, width)], wide.at[d], chunk_sem.at[d]
        )
        copy.start()
        chunks.append(copy)
    groups = BS // 8

    def fetch(source, target, sem, g):
        span = pl.ds(pl.multiple_of(g * 8, 8), 8)
        return pltpu.make_async_copy(source.at[span], target.at[span], sem.at[g])

    loads = [
        pltpu.make_async_copy(fwd, fwd_v, load_sem.at[0]),
        pltpu.make_async_copy(inv, inv_v, load_sem.at[1]),
        pltpu.make_async_copy(mir, mir_v, load_sem.at[2]),
    ]
    for g in range(groups):
        fetch(jacobi, jac_raw, jac_sem, g).start()
    loads[0].start()
    for g in range(groups):
        fetch(op_main, main_raw, main_sem, g).start()
    for g in range(groups):
        fetch(op_mass, mass_raw, mass_sem, g).start()
    loads[1].start()
    loads[2].start()

    barrier = pltpu.get_barrier_semaphore()
    for d in range(1, tm):
        pl.semaphore_signal(barrier, 1, device_id={"tm": me ^ d, "space": plane}, device_id_type=MESH)
    for hop in hops:
        @pl.when(jnp.logical_and(order + hop >= 0, order + hop < total))
        def _():
            pl.semaphore_signal(barrier, 1, device_id=coords(order + hop), device_id_type=MESH)
    row = pl.multiple_of(me * steps, steps)

    def exchange1(i, d, begin):
        return pltpu.make_async_remote_copy(
            src_ref=sends.at[i, d], dst_ref=cols.at[i, pl.ds(begin, steps), :],
            send_sem=send1.at[i * tm + d], recv_sem=recv1.at[i * tm + d],
            device_id={"tm": me ^ d, "space": plane}, device_id_type=MESH,
        )

    def arrival1(i, d):
        return exchange1(i, d, pl.multiple_of((me ^ d) * steps, steps))

    for d, copy in zip(peers, chunks):
        copy.wait()
        for i in range(lines):
            part = wide[d, :, i * LINE:(i + 1) * LINE].astype(bf16)
            if d == 0:
                cols[i, pl.ds(row, steps), :] = part
            else:
                sends[i, d] = part

    held = op_main.shape[2]
    pick_row = lax.broadcasted_iota(jnp.int32, (blocks * 8, 2 * held), 0)
    pick_col = lax.broadcasted_iota(jnp.int32, (blocks * 8, 2 * held), 1)
    late = jnp.where(pick_col >= held, 1, 0)
    same = pick_col - late * held == spot * blocks + pick_row // 8
    for p in range(4):
        hit = jnp.logical_and(same, pick_row % 8 == 2 * p + late)
        pick[p] = jnp.where(hit, 1.0, 0.0).astype(bf16)

    def gather(source, raw, sem, target, start, stop):
        @pl.loop(start, stop)
        def _(g):
            fetch(source, raw, sem, g).wait()
            value = None
            for p in range(4):
                pair = jnp.concatenate([raw[g * 8 + 2 * p], raw[g * 8 + 2 * p + 1]], axis=1)
                term = dot_nt(pick[p], pair)
                value = term if value is None else value + term
            span = pl.ds(pl.multiple_of(g * 8, 8), 8)
            target[:, span, :] = value.reshape(blocks, 8, value.shape[1])

    for hop in hops:
        @pl.when(jnp.logical_or(order - hop < 0, order - hop >= total))
        def _():
            field[pl.ds(BY - hop * lines, lines)] = jnp.zeros((lines, length, LINE), bf16)

    others = sum(
        jnp.where(jnp.logical_and(order + hop >= 0, order + hop < total), 1, 0) for hop in hops
    )
    pl.semaphore_wait(barrier, tm - 1 + others)

    for i in range(lines):
        for d in peers[:-1]:
            exchange1(i, d, row).start()

    zero = jnp.zeros((BS, BS), bf16)
    first_y = lax.rem(spot * lines, BY)

    def assemble(part):
        for i in range(lines):
            for x in range(BX):
                block = i * BX + x
                slot = [picked[block, :, s * BS:(s + 1) * BS].astype(bf16) for s in range(7)]
                span = pl.ds(part * LINE + x * BS, BS)
                along = {x: slot[0], x - 1: slot[1], x + 1: slot[2]}
                weights[i, 0, span, :] = jnp.concatenate(
                    [along.get(j, zero) for j in range(BX)], axis=1
                )
                below, above = slot[3], slot[4]
                if lines != BY:
                    y = first_y + i
                    below = jnp.where(y > 0, below, zero)
                    above = jnp.where(y < BY - 1, above, zero)
                for s, piece in ((1, below), (2, above), (3, slot[5]), (4, slot[6])):
                    weights[i, s, span, :] = jnp.concatenate(
                        [piece if j == x else zero for j in range(BX)], axis=1
                    )

    gather(jacobi, jac_raw, jac_sem, picked_jac, 0, groups)
    for i in range(lines):
        for x in range(BX):
            own = picked_jac[i * BX + x].astype(bf16)
            gains[i, pl.ds(x * BS, BS), :] = jnp.concatenate(
                [own if j == x else zero for j in range(BX)], axis=1
            )

    def halo(hop, i, target):
        index = hops.index(hop) * lines + i
        return pltpu.make_async_remote_copy(
            src_ref=field.at[BY + i], dst_ref=field.at[BY - hop * lines + i],
            send_sem=send2.at[index], recv_sem=recv2.at[index],
            device_id=coords(target), device_id_type=MESH,
        )

    loads[0].wait()
    for i in range(lines):
        gather(op_main, main_raw, main_sem, picked, i * groups // lines, (i + 1) * groups // lines)
        for d in peers[:-1]:
            arrival1(i, d).wait_recv()
        part = cols[i]
        hat = dot_nn(fwd_v[0], part) + dot_nn(fwd_v[1], part)
        rhs[i] = hat
        image = dot_nt(hat.astype(bf16), gains[i])
        first[i] = image
        field[BY + i] = image.astype(bf16)
        for hop in hops:
            @pl.when(jnp.logical_and(order + hop >= 0, order + hop < total))
            def _():
                halo(hop, i, order + hop).start()

    assemble(0)
    gather(op_mass, mass_raw, mass_sem, picked, 0, groups)
    assemble(1)

    def outside(j):
        return j < 0 or j >= lines

    for i in range(lines):
        value = dot_nt(field[BY + i], weights[i, 0])
        for s, j in ((1, i - 1), (2, i + 1)):
            if not outside(j):
                value += dot_nt(field[BY + j], weights[i, s])
        acc[i] = value

    def arrive(hop, i):
        @pl.when(jnp.logical_and(order - hop >= 0, order - hop < total))
        def _():
            halo(hop, i, order - hop).wait_recv()

    if lines != BY:
        for hop in hops:
            for i in range(lines):
                arrive(hop, i)
    loads[1].wait()
    loads[2].wait()
    top = lax.broadcasted_iota(jnp.int32, (half, LINE), 0) == 0
    own_low = coef[0][:, :1]
    own_high = coef[1][:, :1]
    cross = coef[2][:, :1]
    mine = spot * lines

    def exchange3(i, d, begin):
        theirs = pl.multiple_of((me ^ d) * steps, steps)
        return pltpu.make_async_remote_copy(
            src_ref=out_v.at[i, :, pl.ds(theirs, steps), :], dst_ref=out.at[begin + i],
            send_sem=send3.at[i * tm + d], recv_sem=recv3.at[i * tm + d],
            device_id={"tm": me ^ d, "space": plane}, device_id_type=MESH,
        )

    keep = []
    for i in range(lines):
        if lines == BY:
            arrive(1, i)
            arrive(-1, i)
        value = acc[i] + dot_nt(field[i], weights[i, 3])
        value += dot_nt(field[i + 2 * BY], weights[i, 4])
        if lines != BY:
            for s, j in ((1, i - 1), (2, i + 1)):
                if outside(j):
                    value += dot_nt(field[BY + j], weights[i, s])
        mass_re = value[:half, LINE:]
        mass_im = value[half:, LINE:]
        res_re = rhs[i, :half] - value[:half, :LINE] + own_low * mass_re - cross * mass_im
        res_im = rhs[i, half:] - value[half:, :LINE] + own_high * mass_im + cross * mass_re
        residue = jnp.concatenate([res_re.astype(bf16), res_im.astype(bf16)], axis=0)
        second = first[i] + dot_nt(residue, gains[i])
        high = second.astype(bf16)
        low = (second - high.astype(jnp.float32)).astype(bf16)
        mirrored = dot_nn(mir_v[...], high).astype(bf16)
        out_v[i, 0, :half] = high[:half]
        out_v[i, 0, half:] = mirrored[:half]
        out_v[i, 1, :half] = jnp.where(top, 0.0, second[half:]).astype(bf16)
        out_v[i, 1, half:] = mirrored[half:]
        value = dot_nn(inv_v[0], high) + dot_nn(inv_v[1], high) + dot_nn(inv_v[0], low)
        out_v[i, 2] = value.astype(bf16)
        for d in peers[:-1]:
            exchange3(i, d, mine).start()
        copy = pltpu.make_async_copy(
            out_v.at[i, :, pl.ds(row, steps), :], out.at[mine + i], own_sem.at[i]
        )
        copy.start()
        keep.append(copy)

    for i in range(lines):
        for d in peers[:-1]:
            exchange1(i, d, row).wait_send()
    for hop in hops:
        @pl.when(jnp.logical_and(order + hop >= 0, order + hop < total))
        def _():
            for i in range(lines):
                halo(hop, i, order + hop).wait_send()
    for i in range(lines):
        keep[i].wait()
        for d in peers[:-1]:
            exchange3(i, d, mine).wait_send()
            exchange3(i, d, place(me ^ d, tm) * lines).wait_recv()


def widen(packed, real, imag, field):
    for i in range(packed.shape[0]):
        span = slice(i * LINE, (i + 1) * LINE)
        real[:, span] = packed[i, 0].astype(jnp.float32)
        imag[:, span] = packed[i, 1].astype(jnp.float32)
        field[:, span] = packed[i, 2].astype(jnp.float32)


def per_device(tm, space, forcing, op_main, op_mass, jacobi_inv):
    steps, dofs = forcing.shape
    length = steps * tm
    lines = dofs // tm // LINE
    width = lines * LINE
    blocks = lines * BX
    held = op_main.shape[0]
    halos = 2 * (BY // lines) * lines
    bf16, f32 = jnp.bfloat16, jnp.float32
    forward, inverse, mirror, coefs = tables(length)
    any_space = pl.BlockSpec(memory_space=pl.ANY)
    vmem = pl.BlockSpec(memory_space=pltpu.VMEM)
    dma = pltpu.SemaphoreType.DMA
    packed = pl.pallas_call(
        functools.partial(kernel, tm, space, lines),
        out_shape=jax.ShapeDtypeStruct((dofs // LINE, 3, steps, LINE), bf16),
        in_specs=[any_space] * 7 + [vmem],
        out_specs=any_space,
        scratch_shapes=[
            pltpu.VMEM((tm, steps, width), f32),
            pltpu.VMEM((lines, tm, steps, LINE), bf16),
            pltpu.VMEM((lines, length, LINE), bf16),
            pltpu.VMEM((BS, 7 * BS, held), bf16),
            pltpu.VMEM((BS, 7 * BS, held), bf16),
            pltpu.VMEM((BS, BS, held), bf16),
            pltpu.VMEM((4, blocks * 8, 2 * held), bf16),
            pltpu.VMEM((blocks, BS, 7 * BS), f32),
            pltpu.VMEM((blocks, BS, BS), f32),
            pltpu.VMEM((2, length, length), bf16),
            pltpu.VMEM((2, length, length), bf16),
            pltpu.VMEM((length, length), bf16),
            pltpu.VMEM((lines, 5, 2 * LINE, LINE), bf16),
            pltpu.VMEM((lines, LINE, LINE), bf16),
            pltpu.VMEM((lines + 2 * BY, length, LINE), bf16),
            pltpu.VMEM((lines, length, LINE), f32),
            pltpu.VMEM((lines, length, LINE), f32),
            pltpu.VMEM((lines, length, 2 * LINE), f32),
            pltpu.VMEM((lines, 3, length, LINE), bf16),
            dma((3,)), dma((BS // 8,)), dma((BS // 8,)), dma((BS // 8,)), dma((tm,)), dma((lines,)),
            dma((lines * tm,)), dma((lines * tm,)),
            dma((halos,)), dma((halos,)),
            dma((lines * tm,)), dma((lines * tm,)),
        ],
        compiler_params=pltpu.CompilerParams(
            collective_id=0, has_side_effects=True, vmem_limit_bytes=56 * 1024 * 1024
        ),
    )(
        forcing, *(jnp.transpose(op, (1, 2, 0)) for op in (op_main, op_mass, jacobi_inv)),
        jnp.asarray(forward), jnp.asarray(inverse), jnp.asarray(mirror), jnp.asarray(coefs),
    )
    wide = dofs // 4
    out_spec = pl.BlockSpec((steps, wide), lambda step: (0, step))
    return pl.pallas_call(
        widen,
        grid=(4,),
        out_shape=[jax.ShapeDtypeStruct((steps, dofs), f32)] * 3,
        in_specs=[pl.BlockSpec((wide // LINE, 3, steps, LINE), lambda step: (step, 0, 0, 0))],
        out_specs=[out_spec] * 3,
    )(packed)


def solution(mesh):
    in_specs = (
        P("tm", "space"),
        P("space", None, None),
        P("space", None, None),
        P("space", None, None),
    )
    out_specs = (P("tm", "space"), P("tm", "space"), P("tm", "space"))
    body = functools.partial(per_device, mesh.shape["tm"], mesh.shape["space"])
    return jax.shard_map(
        body, mesh=mesh, in_specs=in_specs, out_specs=out_specs, check_vma=False
    )
```

```python
import functools
import math

import jax
import jax.numpy as jnp
import numpy as np
from jax import lax
from jax.experimental import pallas as pl
from jax.experimental.pallas import tpu as pltpu
from jax.sharding import PartitionSpec as P

BS = 64
BX = 4
BY = 4
LINE = BX * BS

alpha_decay = 0.25
MESH = pl.DeviceIdType.MESH


def split_table(table):
    high = table.astype(jnp.bfloat16)
    low = (table - high.astype(np.float64)).astype(jnp.bfloat16)
    return np.stack([high, low])


def tables(length):
    half = length // 2
    ids = np.arange(length)
    freqs = np.arange(half)
    angles = 2.0 * math.pi * ((freqs[:, None] * ids[None, :]) % length) / length
    norm = 1.0 / math.sqrt(length)
    real_rows = np.cos(angles) * norm
    imag_rows = -np.sin(angles) * norm
    imag_rows[0] = np.where(ids % 2 == 0, norm, -norm)
    packed = np.concatenate([real_rows, imag_rows], axis=0)
    decay = alpha_decay ** (ids / length)
    forward = packed * decay[None, :]
    weight = np.full((length,), 2.0)
    weight[0] = 1.0
    weight[half] = 1.0
    inverse = (packed * weight[:, None]).T / decay[:, None]
    mirror = np.zeros((length, length))
    mirror[0, half] = 1.0
    for row in range(1, half):
        mirror[row, half - row] = 1.0
        mirror[half + row, length - row] = -1.0
    modulus = alpha_decay ** (1.0 / length)
    beta = modulus * np.exp(-2j * math.pi * freqs / length)
    beta_high = beta.real.copy()
    beta_high[0] = -modulus
    beta_cross = beta.imag.copy()
    beta_cross[0] = 0.0
    coefs = np.stack([beta.real, beta_high, beta_cross]).astype(np.float32)
    coefs = np.ascontiguousarray(np.broadcast_to(coefs[:, :, None], (3, half, 128)))
    return split_table(forward), split_table(inverse), mirror.astype(jnp.bfloat16), coefs


def place(rank, count):
    quarter = count // 4
    chip = rank // quarter
    return (chip ^ (chip >> 1)) * quarter + rank % quarter


def dot_nn(left, right):
    return jnp.dot(left, right, preferred_element_type=jnp.float32)


def dot_nt(left, right):
    return lax.dot_general(
        left, right, (((1,), (1,)), ((), ())), preferred_element_type=jnp.float32
    )


def kernel(
    tm, space, lines,
    forcing, op_main, op_mass, jacobi, fwd, inv, mir, coef,
    out,
    wide, sends, cols, main_raw, mass_raw, jac_raw, pick, picked, picked_jac, fwd_v, inv_v, mir_v, weights, gains,
    field, rhs, first, acc, out_v,
    load_sem, main_sem, mass_sem, jac_sem, chunk_sem, own_sem,
    send1, recv1, send2, recv2, send3, recv3,
):
    bf16 = jnp.bfloat16
    me = lax.axis_index("tm")
    plane = lax.axis_index("space")
    steps = forcing.shape[0]
    length = steps * tm
    half = length // 2
    width = lines * LINE
    blocks = lines * BX
    reach = BY // lines
    total = tm * space
    spot = place(me, tm)
    order = plane * tm + spot
    hops = [d for m in range(1, reach + 1) for d in (m, -m)]

    def coords(position):
        return {"tm": place(lax.rem(position, tm), tm), "space": position // tm}

    chunks = []
    peers = list(range(tm - 1, -1, -1))
    for d in peers:
        begin = pl.multiple_of(place(me ^ d, tm) * width, width)
        copy = pltpu.make_async_copy(
            forcing.at[:, pl.ds(begin, width)], wide.at[d], chunk_sem.at[d]
        )
        copy.start()
        chunks.append(copy)
    groups = BS // 8

    def fetch(source, target, sem, g):
        span = pl.ds(pl.multiple_of(g * 8, 8), 8)
        return pltpu.make_async_copy(source.at[span], target.at[span], sem.at[g])

    loads = [
        pltpu.make_async_copy(fwd, fwd_v, load_sem.at[0]),
        pltpu.make_async_copy(inv, inv_v, load_sem.at[1]),
        pltpu.make_async_copy(mir, mir_v, load_sem.at[2]),
    ]
    for g in range(groups):
        fetch(jacobi, jac_raw, jac_sem, g).start()
    loads[0].start()
    for g in range(groups):
        fetch(op_main, main_raw, main_sem, g).start()
    for g in range(groups):
        fetch(op_mass, mass_raw, mass_sem, g).start()
    loads[1].start()
    loads[2].start()

    barrier = pltpu.get_barrier_semaphore()
    for d in range(1, tm):
        pl.semaphore_signal(barrier, 1, device_id={"tm": me ^ d, "space": plane}, device_id_type=MESH)
    for hop in hops:
        @pl.when(jnp.logical_and(order + hop >= 0, order + hop < total))
        def _():
            pl.semaphore_signal(barrier, 1, device_id=coords(order + hop), device_id_type=MESH)
    row = pl.multiple_of(me * steps, steps)

    def exchange1(i, d, begin):
        return pltpu.make_async_remote_copy(
            src_ref=sends.at[i, d], dst_ref=cols.at[i, pl.ds(begin, steps), :],
            send_sem=send1.at[i * tm + d], recv_sem=recv1.at[i * tm + d],
            device_id={"tm": me ^ d, "space": plane}, device_id_type=MESH,
        )

    def arrival1(i, d):
        return exchange1(i, d, pl.multiple_of((me ^ d) * steps, steps))

    for d, copy in zip(peers, chunks):
        copy.wait()
        for i in range(lines):
            part = wide[d, :, i * LINE:(i + 1) * LINE].astype(bf16)
            if d == 0:
                cols[i, pl.ds(row, steps), :] = part
            else:
                sends[i, d] = part

    held = op_main.shape[2]
    pick_row = lax.broadcasted_iota(jnp.int32, (2 * blocks, 2 * held), 0)
    pick_col = lax.broadcasted_iota(jnp.int32, (2 * blocks, 2 * held), 1)
    late_row = jnp.where(pick_row >= blocks, 1, 0)
    late_col = jnp.where(pick_col >= held, 1, 0)
    wanted = pick_row - late_row * blocks + spot * blocks == pick_col - late_col * held
    hit = jnp.logical_and(wanted, late_row == late_col)
    pick[...] = jnp.where(hit, 1.0, 0.0).astype(bf16)

    def gather(source, raw, sem, target, start, stop):
        @pl.loop(start, stop)
        def _(g):
            fetch(source, raw, sem, g).wait()
            for p in range(4):
                pair = jnp.concatenate([raw[g * 8 + 2 * p], raw[g * 8 + 2 * p + 1]], axis=1)
                span = pl.ds(pl.multiple_of((g * 4 + p) * 2 * blocks, 2 * blocks), 2 * blocks)
                value = dot_nt(pick[...], pair)
                for t in range(target.shape[0]):
                    part = value[:, t * 128:(t + 1) * 128]
                    target[t, span, :part.shape[1]] = part

    for hop in hops:
        @pl.when(jnp.logical_or(order - hop < 0, order - hop >= total))
        def _():
            field[pl.ds(BY - hop * lines, lines)] = jnp.zeros((lines, length, LINE), bf16)

    others = sum(
        jnp.where(jnp.logical_and(order + hop >= 0, order + hop < total), 1, 0) for hop in hops
    )
    pl.semaphore_wait(barrier, tm - 1 + others)

    for i in range(lines):
        for d in peers[:-1]:
            exchange1(i, d, row).start()

    zero = jnp.zeros((BS, BS), bf16)
    first_y = lax.rem(spot * lines, BY)

    def assemble(part):
        for i in range(lines):
            for x in range(BX):
                block = i * BX + x
                rows = [
                    picked[t, pl.ds(block, BS, stride=blocks), :].astype(bf16) for t in range(4)
                ]
                slot = [rows[s // 2][:, s % 2 * BS:(s % 2 + 1) * BS] for s in range(7)]
                span = pl.ds(part * LINE + x * BS, BS)
                along = {x: slot[0], x - 1: slot[1], x + 1: slot[2]}
                weights[i, 0, span, :] = jnp.concatenate(
                    [along.get(j, zero) for j in range(BX)], axis=1
                )
                below, above = slot[3], slot[4]
                if lines != BY:
                    y = first_y + i
                    below = jnp.where(y > 0, below, zero)
                    above = jnp.where(y < BY - 1, above, zero)
                for s, piece in ((1, below), (2, above), (3, slot[5]), (4, slot[6])):
                    weights[i, s, span, :] = jnp.concatenate(
                        [piece if j == x else zero for j in range(BX)], axis=1
                    )

    gather(jacobi, jac_raw, jac_sem, picked_jac, 0, groups)
    for i in range(lines):
        for x in range(BX):
            own = picked_jac[0, pl.ds(i * BX + x, BS, stride=blocks), :].astype(bf16)[:, :BS]
            gains[i, pl.ds(x * BS, BS), :] = jnp.concatenate(
                [own if j == x else zero for j in range(BX)], axis=1
            )

    def halo(hop, i, target):
        index = hops.index(hop) * lines + i
        return pltpu.make_async_remote_copy(
            src_ref=field.at[BY + i], dst_ref=field.at[BY - hop * lines + i],
            send_sem=send2.at[index], recv_sem=recv2.at[index],
            device_id=coords(target), device_id_type=MESH,
        )

    loads[0].wait()
    for i in range(lines):
        gather(op_main, main_raw, main_sem, picked, i * groups // lines, (i + 1) * groups // lines)
        for d in peers[:-1]:
            arrival1(i, d).wait_recv()
        part = cols[i]
        hat = dot_nn(fwd_v[0], part) + dot_nn(fwd_v[1], part)
        rhs[i] = hat
        image = dot_nt(hat.astype(bf16), gains[i])
        first[i] = image
        field[BY + i] = image.astype(bf16)
        for hop in hops:
            @pl.when(jnp.logical_and(order + hop >= 0, order + hop < total))
            def _():
                halo(hop, i, order + hop).start()

    assemble(0)
    gather(op_mass, mass_raw, mass_sem, picked, 0, groups)
    assemble(1)

    def outside(j):
        return j < 0 or j >= lines

    for i in range(lines):
        value = dot_nt(field[BY + i], weights[i, 0])
        for s, j in ((1, i - 1), (2, i + 1)):
            if not outside(j):
                value += dot_nt(field[BY + j], weights[i, s])
        acc[i] = value

    def arrive(hop, i):
        @pl.when(jnp.logical_and(order - hop >= 0, order - hop < total))
        def _():
            halo(hop, i, order - hop).wait_recv()

    if lines != BY:
        for hop in hops:
            for i in range(lines):
                arrive(hop, i)
    loads[1].wait()
    loads[2].wait()
    top = lax.broadcasted_iota(jnp.int32, (half, LINE), 0) == 0
    own_low = coef[0][:, :1]
    own_high = coef[1][:, :1]
    cross = coef[2][:, :1]
    mine = spot * lines

    def exchange3(i, d, begin):
        theirs = pl.multiple_of((me ^ d) * steps, steps)
        return pltpu.make_async_remote_copy(
            src_ref=out_v.at[i, :, pl.ds(theirs, steps), :], dst_ref=out.at[begin + i],
            send_sem=send3.at[i * tm + d], recv_sem=recv3.at[i * tm + d],
            device_id={"tm": me ^ d, "space": plane}, device_id_type=MESH,
        )

    keep = []
    for i in range(lines):
        if lines == BY:
            arrive(1, i)
            arrive(-1, i)
        value = acc[i] + dot_nt(field[i], weights[i, 3])
        value += dot_nt(field[i + 2 * BY], weights[i, 4])
        if lines != BY:
            for s, j in ((1, i - 1), (2, i + 1)):
                if outside(j):
                    value += dot_nt(field[BY + j], weights[i, s])
        mass_re = value[:half, LINE:]
        mass_im = value[half:, LINE:]
        res_re = rhs[i, :half] - value[:half, :LINE] + own_low * mass_re - cross * mass_im
        res_im = rhs[i, half:] - value[half:, :LINE] + own_high * mass_im + cross * mass_re
        residue = jnp.concatenate([res_re.astype(bf16), res_im.astype(bf16)], axis=0)
        second = first[i] + dot_nt(residue, gains[i])
        high = second.astype(bf16)
        low = (second - high.astype(jnp.float32)).astype(bf16)
        mirrored = dot_nn(mir_v[...], high).astype(bf16)
        out_v[i, 0, :half] = high[:half]
        out_v[i, 0, half:] = mirrored[:half]
        out_v[i, 1, :half] = jnp.where(top, 0.0, second[half:]).astype(bf16)
        out_v[i, 1, half:] = mirrored[half:]
        value = dot_nn(inv_v[0], high) + dot_nn(inv_v[1], high) + dot_nn(inv_v[0], low)
        out_v[i, 2] = value.astype(bf16)
        for d in peers[:-1]:
            exchange3(i, d, mine).start()
        copy = pltpu.make_async_copy(
            out_v.at[i, :, pl.ds(row, steps), :], out.at[mine + i], own_sem.at[i]
        )
        copy.start()
        keep.append(copy)

    for i in range(lines):
        for d in peers[:-1]:
            exchange1(i, d, row).wait_send()
    for hop in hops:
        @pl.when(jnp.logical_and(order + hop >= 0, order + hop < total))
        def _():
            for i in range(lines):
                halo(hop, i, order + hop).wait_send()
    for i in range(lines):
        keep[i].wait()
        for d in peers[:-1]:
            exchange3(i, d, mine).wait_send()
            exchange3(i, d, place(me ^ d, tm) * lines).wait_recv()


def widen(packed, real, imag, field):
    for i in range(packed.shape[0]):
        span = slice(i * LINE, (i + 1) * LINE)
        real[:, span] = packed[i, 0].astype(jnp.float32)
        imag[:, span] = packed[i, 1].astype(jnp.float32)
        field[:, span] = packed[i, 2].astype(jnp.float32)


def per_device(tm, space, forcing, op_main, op_mass, jacobi_inv):
    steps, dofs = forcing.shape
    length = steps * tm
    lines = dofs // tm // LINE
    width = lines * LINE
    blocks = lines * BX
    held = op_main.shape[0]
    halos = 2 * (BY // lines) * lines
    bf16, f32 = jnp.bfloat16, jnp.float32
    forward, inverse, mirror, coefs = tables(length)
    any_space = pl.BlockSpec(memory_space=pl.ANY)
    vmem = pl.BlockSpec(memory_space=pltpu.VMEM)
    dma = pltpu.SemaphoreType.DMA
    packed = pl.pallas_call(
        functools.partial(kernel, tm, space, lines),
        out_shape=jax.ShapeDtypeStruct((dofs // LINE, 3, steps, LINE), bf16),
        in_specs=[any_space] * 7 + [vmem],
        out_specs=any_space,
        scratch_shapes=[
            pltpu.VMEM((tm, steps, width), f32),
            pltpu.VMEM((lines, tm, steps, LINE), bf16),
            pltpu.VMEM((lines, length, LINE), bf16),
            pltpu.VMEM((BS, 7 * BS, held), bf16),
            pltpu.VMEM((BS, 7 * BS, held), bf16),
            pltpu.VMEM((BS, BS, held), bf16),
            pltpu.VMEM((2 * blocks, 2 * held), bf16),
            pltpu.VMEM((4, BS * blocks, 128), f32),
            pltpu.VMEM((1, BS * blocks, 128), f32),
            pltpu.VMEM((2, length, length), bf16),
            pltpu.VMEM((2, length, length), bf16),
            pltpu.VMEM((length, length), bf16),
            pltpu.VMEM((lines, 5, 2 * LINE, LINE), bf16),
            pltpu.VMEM((lines, LINE, LINE), bf16),
            pltpu.VMEM((lines + 2 * BY, length, LINE), bf16),
            pltpu.VMEM((lines, length, LINE), f32),
            pltpu.VMEM((lines, length, LINE), f32),
            pltpu.VMEM((lines, length, 2 * LINE), f32),
            pltpu.VMEM((lines, 3, length, LINE), bf16),
            dma((3,)), dma((BS // 8,)), dma((BS // 8,)), dma((BS // 8,)), dma((tm,)), dma((lines,)),
            dma((lines * tm,)), dma((lines * tm,)),
            dma((halos,)), dma((halos,)),
            dma((lines * tm,)), dma((lines * tm,)),
        ],
        compiler_params=pltpu.CompilerParams(
            collective_id=0, has_side_effects=True, vmem_limit_bytes=56 * 1024 * 1024
        ),
    )(
        forcing, *(jnp.transpose(op, (1, 2, 0)) for op in (op_main, op_mass, jacobi_inv)),
        jnp.asarray(forward), jnp.asarray(inverse), jnp.asarray(mirror), jnp.asarray(coefs),
    )
    wide = dofs // 4
    out_spec = pl.BlockSpec((steps, wide), lambda step: (0, step))
    return pl.pallas_call(
        widen,
        grid=(4,),
        out_shape=[jax.ShapeDtypeStruct((steps, dofs), f32)] * 3,
        in_specs=[pl.BlockSpec((wide // LINE, 3, steps, LINE), lambda step: (step, 0, 0, 0))],
        out_specs=[out_spec] * 3,
    )(packed)


def solution(mesh):
    in_specs = (
        P("tm", "space"),
        P("space", None, None),
        P("space", None, None),
        P("space", None, None),
    )
    out_specs = (P("tm", "space"), P("tm", "space"), P("tm", "space"))
    body = functools.partial(per_device, mesh.shape["tm"], mesh.shape["space"])
    return jax.shard_map(
        body, mesh=mesh, in_specs=in_specs, out_specs=out_specs, check_vma=False
    )
```

```python
import functools
import math

import jax
import jax.numpy as jnp
import numpy as np
from jax import lax
from jax.experimental import pallas as pl
from jax.experimental.pallas import tpu as pltpu
from jax.sharding import PartitionSpec as P

BS = 64
BX = 4
BY = 4
LINE = BX * BS

alpha_decay = 0.25
MESH = pl.DeviceIdType.MESH


def split_table(table):
    high = table.astype(jnp.bfloat16)
    low = (table - high.astype(np.float64)).astype(jnp.bfloat16)
    return np.stack([high, low])


def tables(length):
    half = length // 2
    ids = np.arange(length)
    freqs = np.arange(half)
    angles = 2.0 * math.pi * ((freqs[:, None] * ids[None, :]) % length) / length
    norm = 1.0 / math.sqrt(length)
    real_rows = np.cos(angles) * norm
    imag_rows = -np.sin(angles) * norm
    imag_rows[0] = np.where(ids % 2 == 0, norm, -norm)
    packed = np.concatenate([real_rows, imag_rows], axis=0)
    decay = alpha_decay ** (ids / length)
    forward = packed * decay[None, :]
    weight = np.full((length,), 2.0)
    weight[0] = 1.0
    weight[half] = 1.0
    inverse = (packed * weight[:, None]).T / decay[:, None]
    mirror = np.zeros((length, length))
    mirror[0, half] = 1.0
    for row in range(1, half):
        mirror[row, half - row] = 1.0
        mirror[half + row, length - row] = -1.0
    modulus = alpha_decay ** (1.0 / length)
    beta = modulus * np.exp(-2j * math.pi * freqs / length)
    beta_high = beta.real.copy()
    beta_high[0] = -modulus
    beta_cross = beta.imag.copy()
    beta_cross[0] = 0.0
    coefs = np.stack([beta.real, beta_high, beta_cross]).astype(np.float32)
    coefs = np.ascontiguousarray(np.broadcast_to(coefs[:, :, None], (3, half, 128)))
    return split_table(forward), split_table(inverse), mirror.astype(jnp.bfloat16), coefs


def place(rank, count):
    quarter = count // 4
    chip = rank // quarter
    return (chip ^ (chip >> 1)) * quarter + rank % quarter


def dot_nn(left, right):
    return jnp.dot(left, right, preferred_element_type=jnp.float32)


def dot_nt(left, right):
    return lax.dot_general(
        left, right, (((1,), (1,)), ((), ())), preferred_element_type=jnp.float32
    )


def kernel(
    tm, space, lines,
    forcing, op_main, op_mass, jacobi, fwd, inv, mir, coef,
    out,
    wide, sends, cols, main_raw, mass_raw, jac_raw, pick, picked, picked_jac, fwd_v, inv_v, mir_v, weights, gains,
    field, rhs, first, acc, out_v,
    load_sem, main_sem, mass_sem, jac_sem, chunk_sem, own_sem,
    send1, recv1, send2, recv2, send3, recv3,
):
    bf16 = jnp.bfloat16
    me = lax.axis_index("tm")
    plane = lax.axis_index("space")
    steps = forcing.shape[0]
    length = steps * tm
    half = length // 2
    width = lines * LINE
    blocks = lines * BX
    reach = BY // lines
    total = tm * space
    spot = place(me, tm)
    order = plane * tm + spot
    hops = [d for m in range(1, reach + 1) for d in (m, -m)]

    def coords(position):
        return {"tm": place(lax.rem(position, tm), tm), "space": position // tm}

    chunks = []
    peers = list(range(tm - 1, -1, -1))
    for d in peers:
        begin = pl.multiple_of(place(me ^ d, tm) * width, width)
        copy = pltpu.make_async_copy(
            forcing.at[:, pl.ds(begin, width)], wide.at[d], chunk_sem.at[d]
        )
        copy.start()
        chunks.append(copy)
    groups = BS // 8

    def fetch(source, target, sem, g):
        span = pl.ds(pl.multiple_of(g * 8, 8), 8)
        return pltpu.make_async_copy(source.at[span], target.at[span], sem.at[g])

    loads = [
        pltpu.make_async_copy(fwd, fwd_v, load_sem.at[0]),
        pltpu.make_async_copy(inv, inv_v, load_sem.at[1]),
        pltpu.make_async_copy(mir, mir_v, load_sem.at[2]),
    ]
    for g in range(groups):
        fetch(jacobi, jac_raw, jac_sem, g).start()
    loads[0].start()
    for g in range(groups):
        fetch(op_main, main_raw, main_sem, g).start()
    for g in range(groups):
        fetch(op_mass, mass_raw, mass_sem, g).start()
    loads[1].start()
    loads[2].start()

    barrier = pltpu.get_barrier_semaphore()
    for d in range(1, tm):
        pl.semaphore_signal(barrier, 1, device_id={"tm": me ^ d, "space": plane}, device_id_type=MESH)
    for hop in hops:
        @pl.when(jnp.logical_and(order + hop >= 0, order + hop < total))
        def _():
            pl.semaphore_signal(barrier, 1, device_id=coords(order + hop), device_id_type=MESH)
    row = pl.multiple_of(me * steps, steps)

    def exchange1(i, d, begin):
        return pltpu.make_async_remote_copy(
            src_ref=sends.at[i, d], dst_ref=cols.at[i, pl.ds(begin, steps), :],
            send_sem=send1.at[i * tm + d], recv_sem=recv1.at[i * tm + d],
            device_id={"tm": me ^ d, "space": plane}, device_id_type=MESH,
        )

    def arrival1(i, d):
        return exchange1(i, d, pl.multiple_of((me ^ d) * steps, steps))

    for d, copy in zip(peers, chunks):
        copy.wait()
        for i in range(lines):
            part = wide[d, :, i * LINE:(i + 1) * LINE].astype(bf16)
            if d == 0:
                cols[i, pl.ds(row, steps), :] = part
            else:
                sends[i, d] = part

    held = op_main.shape[2]
    pick_row = lax.broadcasted_iota(jnp.int32, (2 * blocks, 2 * held), 0)
    pick_col = lax.broadcasted_iota(jnp.int32, (2 * blocks, 2 * held), 1)
    late_row = jnp.where(pick_row >= blocks, 1, 0)
    late_col = jnp.where(pick_col >= held, 1, 0)
    wanted = pick_row - late_row * blocks + spot * blocks == pick_col - late_col * held
    hit = jnp.logical_and(wanted, late_row == late_col)
    pick[...] = jnp.where(hit, 1.0, 0.0).astype(bf16)

    def gather(source, raw, sem, target, start, stop):
        @pl.loop(start, stop)
        def _(g):
            fetch(source, raw, sem, g).wait()
            for p in range(4):
                pair = jnp.concatenate([raw[g * 8 + 2 * p], raw[g * 8 + 2 * p + 1]], axis=1)
                span = pl.ds(pl.multiple_of((g * 4 + p) * 2 * blocks, 2 * blocks), 2 * blocks)
                value = dot_nt(pick[...], pair)
                for t in range(target.shape[0]):
                    part = value[:, t * 128:(t + 1) * 128]
                    target[t, span, :part.shape[1]] = part

    for hop in hops:
        @pl.when(jnp.logical_or(order - hop < 0, order - hop >= total))
        def _():
            field[pl.ds(BY - hop * lines, lines)] = jnp.zeros((lines, length, LINE), bf16)

    others = sum(
        jnp.where(jnp.logical_and(order + hop >= 0, order + hop < total), 1, 0) for hop in hops
    )
    pl.semaphore_wait(barrier, tm - 1 + others)

    for i in range(lines):
        for d in peers[:-1]:
            exchange1(i, d, row).start()

    zero = jnp.zeros((BS, BS), bf16)
    first_y = lax.rem(spot * lines, BY)

    def assemble(part):
        for i in range(lines):
            for x in range(BX):
                block = i * BX + x
                rows = [
                    picked[t, pl.ds(block, BS, stride=blocks), :].astype(bf16) for t in range(4)
                ]
                slot = [rows[s // 2][:, s % 2 * BS:(s % 2 + 1) * BS] for s in range(7)]
                span = pl.ds(part * LINE + x * BS, BS)
                along = {x: slot[0], x - 1: slot[1], x + 1: slot[2]}
                weights[i, 0, span, :] = jnp.concatenate(
                    [along.get(j, zero) for j in range(BX)], axis=1
                )
                below, above = slot[3], slot[4]
                if lines != BY:
                    y = first_y + i
                    below = jnp.where(y > 0, below, zero)
                    above = jnp.where(y < BY - 1, above, zero)
                for s, piece in ((1, below), (2, above), (3, slot[5]), (4, slot[6])):
                    weights[i, s, span, :] = jnp.concatenate(
                        [piece if j == x else zero for j in range(BX)], axis=1
                    )

    gather(jacobi, jac_raw, jac_sem, picked_jac, 0, groups)
    for i in range(lines):
        for x in range(BX):
            own = picked_jac[0, pl.ds(i * BX + x, BS, stride=blocks), :].astype(bf16)[:, :BS]
            gains[i, pl.ds(x * BS, BS), :] = jnp.concatenate(
                [own if j == x else zero for j in range(BX)], axis=1
            )

    def halo(hop, i, target):
        index = hops.index(hop) * lines + i
        return pltpu.make_async_remote_copy(
            src_ref=field.at[BY + i], dst_ref=field.at[BY - hop * lines + i],
            send_sem=send2.at[index], recv_sem=recv2.at[index],
            device_id=coords(target), device_id_type=MESH,
        )

    loads[0].wait()
    for i in range(lines):
        gather(op_main, main_raw, main_sem, picked, i * groups // lines, (i + 1) * groups // lines)
        for d in peers[:-1]:
            arrival1(i, d).wait_recv()
        part = cols[i]
        hat = dot_nn(fwd_v[0], part) + dot_nn(fwd_v[1], part)
        rhs[i] = hat
        image = dot_nt(hat.astype(bf16), gains[i])
        first[i] = image
        field[BY + i] = image.astype(bf16)
        for hop in hops:
            @pl.when(jnp.logical_and(order + hop >= 0, order + hop < total))
            def _():
                halo(hop, i, order + hop).start()

    assemble(0)
    gather(op_mass, mass_raw, mass_sem, picked, 0, groups)
    assemble(1)

    def outside(j):
        return j < 0 or j >= lines

    for i in range(lines):
        value = dot_nt(field[BY + i], weights[i, 0])
        for s, j in ((1, i - 1), (2, i + 1)):
            if not outside(j):
                value += dot_nt(field[BY + j], weights[i, s])
        acc[i] = value

    def arrive(hop, i):
        @pl.when(jnp.logical_and(order - hop >= 0, order - hop < total))
        def _():
            halo(hop, i, order - hop).wait_recv()

    if lines != BY:
        for hop in hops:
            for i in range(lines):
                arrive(hop, i)
    loads[1].wait()
    loads[2].wait()
    top = lax.broadcasted_iota(jnp.int32, (half, LINE), 0) == 0
    own_low = coef[0][:, :1]
    own_high = coef[1][:, :1]
    cross = coef[2][:, :1]
    mine = spot * lines

    def exchange3(i, d, begin):
        theirs = pl.multiple_of((me ^ d) * steps, steps)
        return pltpu.make_async_remote_copy(
            src_ref=out_v.at[i, :, pl.ds(theirs, steps), :], dst_ref=out.at[begin + i],
            send_sem=send3.at[i * tm + d], recv_sem=recv3.at[i * tm + d],
            device_id={"tm": me ^ d, "space": plane}, device_id_type=MESH,
        )

    keep = []
    for i in range(lines):
        if lines == BY:
            arrive(1, i)
            arrive(-1, i)
        value = acc[i] + dot_nt(field[i], weights[i, 3])
        value += dot_nt(field[i + 2 * BY], weights[i, 4])
        if lines != BY:
            for s, j in ((1, i - 1), (2, i + 1)):
                if outside(j):
                    value += dot_nt(field[BY + j], weights[i, s])
        mass_re = value[:half, LINE:]
        mass_im = value[half:, LINE:]
        res_re = rhs[i, :half] - value[:half, :LINE] + own_low * mass_re - cross * mass_im
        res_im = rhs[i, half:] - value[half:, :LINE] + own_high * mass_im + cross * mass_re
        residue = jnp.concatenate([res_re.astype(bf16), res_im.astype(bf16)], axis=0)
        second = first[i] + dot_nt(residue, gains[i])
        high = second.astype(bf16)
        low = (second - high.astype(jnp.float32)).astype(bf16)
        mirrored = dot_nn(mir_v[...], high).astype(bf16)
        out_v[i, 0, :half] = high[:half]
        out_v[i, 0, half:] = mirrored[:half]
        out_v[i, 1, :half] = jnp.where(top, 0.0, second[half:]).astype(bf16)
        out_v[i, 1, half:] = mirrored[half:]
        value = dot_nn(inv_v[0], high) + dot_nn(inv_v[1], high) + dot_nn(inv_v[0], low)
        out_v[i, 2] = value.astype(bf16)
        for d in peers[:-1]:
            exchange3(i, d, mine).start()
        copy = pltpu.make_async_copy(
            out_v.at[i, :, pl.ds(row, steps), :], out.at[mine + i], own_sem.at[i]
        )
        copy.start()
        keep.append(copy)

    for i in range(lines):
        for d in peers[:-1]:
            exchange1(i, d, row).wait_send()
    for hop in hops:
        @pl.when(jnp.logical_and(order + hop >= 0, order + hop < total))
        def _():
            for i in range(lines):
                halo(hop, i, order + hop).wait_send()
    for i in range(lines):
        keep[i].wait()
        for d in peers[:-1]:
            exchange3(i, d, mine).wait_send()
            exchange3(i, d, place(me ^ d, tm) * lines).wait_recv()


def widen(packed, real, imag, field):
    for i in range(packed.shape[0]):
        span = slice(i * LINE, (i + 1) * LINE)
        real[:, span] = packed[i, 0].astype(jnp.float32)
        imag[:, span] = packed[i, 1].astype(jnp.float32)
        field[:, span] = packed[i, 2].astype(jnp.float32)


def per_device(tm, space, forcing, op_main, op_mass, jacobi_inv):
    steps, dofs = forcing.shape
    length = steps * tm
    lines = dofs // tm // LINE
    width = lines * LINE
    blocks = lines * BX
    held = op_main.shape[0]
    halos = 2 * (BY // lines) * lines
    bf16, f32 = jnp.bfloat16, jnp.float32
    forward, inverse, mirror, coefs = tables(length)
    any_space = pl.BlockSpec(memory_space=pl.ANY)
    vmem = pl.BlockSpec(memory_space=pltpu.VMEM)
    dma = pltpu.SemaphoreType.DMA
    packed = pl.pallas_call(
        functools.partial(kernel, tm, space, lines),
        out_shape=jax.ShapeDtypeStruct((dofs // LINE, 3, steps, LINE), bf16),
        in_specs=[any_space] * 7 + [vmem],
        out_specs=any_space,
        scratch_shapes=[
            pltpu.VMEM((tm, steps, width), f32),
            pltpu.VMEM((lines, tm, steps, LINE), bf16),
            pltpu.VMEM((lines, length, LINE), bf16),
            pltpu.VMEM((BS, 7 * BS, held), bf16),
            pltpu.VMEM((BS, 7 * BS, held), bf16),
            pltpu.VMEM((BS, BS, held), bf16),
            pltpu.VMEM((2 * blocks, 2 * held), bf16),
            pltpu.VMEM((4, BS * blocks, 128), f32),
            pltpu.VMEM((1, BS * blocks, 128), f32),
            pltpu.VMEM((2, length, length), bf16),
            pltpu.VMEM((2, length, length), bf16),
            pltpu.VMEM((length, length), bf16),
            pltpu.VMEM((lines, 5, 2 * LINE, LINE), bf16),
            pltpu.VMEM((lines, LINE, LINE), bf16),
            pltpu.VMEM((lines + 2 * BY, length, LINE), bf16),
            pltpu.VMEM((lines, length, LINE), f32),
            pltpu.VMEM((lines, length, LINE), f32),
            pltpu.VMEM((lines, length, 2 * LINE), f32),
            pltpu.VMEM((lines, 3, length, LINE), bf16),
            dma((3,)), dma((BS // 8,)), dma((BS // 8,)), dma((BS // 8,)), dma((tm,)), dma((lines,)),
            dma((lines * tm,)), dma((lines * tm,)),
            dma((halos,)), dma((halos,)),
            dma((lines * tm,)), dma((lines * tm,)),
        ],
        compiler_params=pltpu.CompilerParams(
            collective_id=0, has_side_effects=True, vmem_limit_bytes=56 * 1024 * 1024
        ),
    )(
        forcing, *(jnp.transpose(op, (1, 2, 0)) for op in (op_main, op_mass, jacobi_inv)),
        jnp.asarray(forward), jnp.asarray(inverse), jnp.asarray(mirror), jnp.asarray(coefs),
    )
    wide = dofs // 2
    out_spec = pl.BlockSpec((steps, wide), lambda step: (0, step))
    return pl.pallas_call(
        widen,
        grid=(2,),
        out_shape=[jax.ShapeDtypeStruct((steps, dofs), f32)] * 3,
        in_specs=[pl.BlockSpec((wide // LINE, 3, steps, LINE), lambda step: (step, 0, 0, 0))],
        out_specs=[out_spec] * 3,
    )(packed)


def solution(mesh):
    in_specs = (
        P("tm", "space"),
        P("space", None, None),
        P("space", None, None),
        P("space", None, None),
    )
    out_specs = (P("tm", "space"), P("tm", "space"), P("tm", "space"))
    body = functools.partial(per_device, mesh.shape["tm"], mesh.shape["space"])
    return jax.shard_map(
        body, mesh=mesh, in_specs=in_specs, out_specs=out_specs, check_vma=False
    )
```
